32 devices in a mesh: dp: 16 (over z, y, x), mp: 2 (over core).
Axes of the slice: x: 2, y: 2, z: 4, core: 2. Of those that a mesh axis runs over, the one named last changes fastest.
Arguments:
- tokens: bfloat16 [128, 8192], P('mp', 'dp'), may hold values from -6 to 6
- norm_gain: float32 [8192], replicated, may hold values from 0.25 to 1.75
- query_weight: bfloat16 [8192, 2048], P(None, 'dp'), may hold values from -0.0625 to 0.0625
- out_weight: bfloat16 [2048, 8192], P(None, 'dp'), may hold values from -0.125 to 0.125
- gate_scalar: float32 [1], replicated, may hold values from 0.4 to 1.5
- image_keys: bfloat16 [32, 64, 2048], P('mp', None, 'dp'), may hold values from -260 to 260
- image_values: bfloat16 [32, 64, 2048], P('mp', None, 'dp'), may hold values from -6 to 6
- active_image: int32 [32, 4], replicated, may hold values from 0 to 31
- image_slot: int32 [32], replicated, may hold values from 0 to 31, each once
Outputs:
- mixed: bfloat16 [128, 8192], P('mp', 'dp')
The draws below stay inside these ranges and needn't reach their ends.
Inputs may be any that keep to these rules, and one draw needn't show every extreme that they name: `image_slot`: each slot 0 to 31 once.
All inputs are finite; a program needn't handle non-finite values.
Results may differ from the reference program's by a relative error of at most 0.0047.
Values may be sent and summed in bfloat16 or wider, within the bound.
No kernel may reach another device: no remote copies, remote signals or barrier semaphores. Data moves between devices by JAX's collectives and lax.ppermute only.
A program may use at most 64 MiB of HBM per device.

```python
import math
import jax
import jax.numpy as jnp
import numpy as np
from jax import lax

D = 8192
DH = 128
VT = 64
STEPS = 4
HEADS = 16
SEQS = 32
ROWS = 128
IMAGES = 32


def draw_image_keys(key, part):
    first = jax.random.fold_in(jax.random.fold_in(key, 17), 0)
    shape = (IMAGES, VT, HEADS * DH)
    return jax.random.normal(first, shape, jnp.float32).astype(jnp.bfloat16)


def plant(drawn, key, smallest, top_value):
    place = [jax.random.randint(jax.random.fold_in(key, axis), (), 0, length) for axis, length in enumerate(drawn.shape)]
    widest = drawn.shape.index(max(drawn.shape))
    next_to = place[:widest] + [(place[widest] + 1) % drawn.shape[widest]] + place[widest + 1:]
    return drawn.at[tuple(place)].set(smallest).at[tuple(next_to)].set(top_value)


def levels(own_key, extent, cuts, least, high):
    loudness = 1.0
    for dim, parts in cuts:
        steps = jax.random.uniform(jax.random.fold_in(jax.random.fold_in(own_key, 6), dim), (parts,), jnp.float32, least / len(cuts), high / len(cuts))
        loudness = loudness * jnp.repeat(jnp.exp(steps), extent[dim] // parts).reshape((-1,) + (1,) * (len(extent) - 1 - dim))
    return loudness


def rank_table(count, skew):
    loads = [(1 << 20) // math.isqrt(grade ** skew) + 1 for grade in range(1, count + 1)]
    deviation = 1 + sum(loads) // (1 << 30)
    return np.cumsum(np.array([max(1, weight // deviation) for weight in loads]))


def ranked(rng, shape, count, skew):
    grid = rank_table(count, skew)
    pick = jax.random.randint(jax.random.fold_in(rng, 1), shape, 0, int(grid[count - 1]))
    rank = jnp.searchsorted(jnp.asarray(grid, jnp.int32), pick, side="right")
    return jax.random.permutation(jax.random.fold_in(rng, 2), count)[rank].astype(jnp.int32)


def normal_values(rng, shape, deviation, reach, shards=(), held_as=jnp.bfloat16):
    level = levels(rng, shape, shards, -0.22, 0.18) if shards else 1.0
    drawn = jax.random.normal(rng, shape, jnp.float32) * deviation * level
    return jnp.minimum(jnp.maximum(drawn, -reach), reach).astype(held_as)


def setup_inputs(seed: int = 0) -> dict:
    keys = jax.random.split(jax.random.key(seed), 10)
    return {
        "tokens": normal_values(keys[0], (ROWS, D), 1.0, 6.0, ((0, 2), (1, 16))),
        "norm_gain": jnp.clip(1.0 + 0.15 * jax.random.normal(keys[1], (D,), jnp.float32), 0.25, 1.75),
        "query_weight": normal_values(keys[2], (D, HEADS * DH), D ** -0.5, 0.0625, ((1, 16),)),
        "out_weight": normal_values(keys[3], (HEADS * DH, D), (HEADS * DH) ** -0.5, 0.125, ((1, 16),)),
        "gate_scalar": jnp.clip(jax.random.uniform(keys[4], (1,), jnp.float32, 0.4, 1.5), 0.4, 1.5),
        "image_keys": draw_image_keys(jax.random.fold_in(keys[9], 71), 0),
        "image_values": normal_values(keys[6], (IMAGES, VT, HEADS * DH), 1.0, 6.0, ((0, 2), (2, 16))),
        "active_image": plant(ranked(keys[7], (SEQS, STEPS), IMAGES, 2), jax.random.fold_in(keys[7], 3), 0, IMAGES - 1).astype(jnp.int32),
        "image_slot": jax.random.permutation(keys[8], IMAGES).astype(jnp.int32),
    }


epsilon = 1e-05

def reference(tokens, norm_gain, query_weight, out_weight, gate_scalar, image_keys, image_values, active_image, image_slot):
    widened = tokens.astype(jnp.float32)
    average = lax.optimization_barrier(jnp.mean(widened, axis=1, keepdims=True))
    centred = widened - average
    variance = lax.optimization_barrier(jnp.mean(centred * centred, axis=1, keepdims=True))
    normed = (centred * lax.rsqrt(variance + epsilon) * norm_gain).astype(jnp.bfloat16)
    queries = jnp.dot(normed, query_weight, preferred_element_type=jnp.float32).astype(jnp.bfloat16)
    wanted = image_slot[active_image.reshape(-1)]

    def one_head(head_index):
        offset = head_index * DH
        head_queries = lax.dynamic_slice_in_dim(queries, offset, DH, 1).astype(jnp.float32)
        head_keys = lax.dynamic_slice_in_dim(image_keys, offset, DH, 2)[wanted].astype(jnp.float32)
        head_values = lax.dynamic_slice_in_dim(image_values, offset, DH, 2)[wanted].astype(jnp.float32)
        scores = jnp.einsum('rd,rtd->rt', head_queries, head_keys) * DH ** (-0.5)
        largest = lax.optimization_barrier(jnp.max(scores, axis=1, keepdims=True))
        expo = jnp.exp(scores - largest)
        totals = lax.optimization_barrier(jnp.sum(expo, axis=1, keepdims=True))
        rounded = lax.optimization_barrier((expo / totals).astype(jnp.bfloat16))
        return jnp.einsum('rt,rtd->rd', rounded.astype(jnp.float32), head_values)
    outputs = lax.map(one_head, jnp.arange(HEADS, dtype=jnp.int32))
    attended = jnp.transpose(outputs, (1, 0, 2)).reshape(ROWS, HEADS * DH).astype(jnp.bfloat16)
    projected = jnp.dot(attended, out_weight, preferred_element_type=jnp.float32)
    return (widened + jnp.tanh(gate_scalar[0]) * projected).astype(jnp.bfloat16)
```

```python
import functools

import jax
import jax.numpy as jnp
from jax import lax
from jax.experimental import pallas as pl
from jax.experimental.pallas import tpu as pltpu
from jax.sharding import PartitionSpec as P

epsilon = 1e-05


VMEM = pl.BlockSpec(memory_space=pltpu.VMEM)
SMEM = pl.BlockSpec(memory_space=pltpu.SMEM)


def masks(size):
    low = 1 << ((size.bit_length() - 1) // 2)
    far = [0] + [low * i for i in reversed(range(1, size // low))]
    near = [0] + list(reversed(range(1, low)))
    return far, near


def exchange(x, axis, size, mask):
    return lax.ppermute(x, axis, [(i, i ^ mask) for i in range(size)])


def gather(x, axis, size):
    far, near = masks(size)
    column = jnp.stack([x] + [exchange(x, axis, size, m) for m in far[1:]])
    return [column] + [exchange(column, axis, size, m) for m in near[1:]]


def sources(me, size):
    far, near = masks(size)
    return [(j, i, jnp.bitwise_xor(me, a | b)) for j, b in enumerate(near) for i, a in enumerate(far)]


def slot_kernel(place_ref, active_ref, slot_ref, out_ref):
    rows = out_ref.shape[0]
    steps = active_ref.shape[1]
    base = place_ref[1] * (rows // steps)
    lane = out_ref.shape[1]
    index = lax.broadcasted_iota(jnp.int32, (8, lane), 0)
    for tile in range(rows // 8):
        block = jnp.zeros((8, lane), jnp.int32)
        for r in range(8):
            row = tile * 8 + r
            block = jnp.where(index == r, slot_ref[active_ref[base + row // steps, row % steps]], block)
        out_ref[tile * 8 : tile * 8 + 8, :] = block


def attend_kernel(dp, mp, place_ref, *refs):
    near = len(masks(dp)[1])
    groups, refs = refs[:near], refs[near:]
    gain_ref, query_ref, wanted_ref = refs[:3]
    keys, values = refs[3 : 3 + mp], refs[3 + mp : 3 + 2 * mp]
    out_ref = refs[-1]
    _, rows, wide = groups[0].shape
    model = dp * wide
    order = sources(place_ref[0], dp)

    total = jnp.zeros((rows, 128), jnp.float32)
    for j, i, _ in order:
        for c in range(wide // 128):
            total += groups[j][i, :, c * 128 : c * 128 + 128].astype(jnp.float32)
    average = jnp.sum(total, axis=1, keepdims=True) * (1.0 / model)
    total = jnp.zeros((rows, 128), jnp.float32)
    for j, i, _ in order:
        for c in range(wide // 128):
            centred = groups[j][i, :, c * 128 : c * 128 + 128].astype(jnp.float32) - average
            total += centred * centred
    variance = jnp.sum(total, axis=1, keepdims=True) * (1.0 / model)
    scale = lax.rsqrt(variance + epsilon)

    queries = jnp.zeros((rows, out_ref.shape[1]), jnp.float32)
    for j, i, source in order:
        centred = groups[j][i].astype(jnp.float32) - average
        normed = (centred * scale * gain_ref[pl.ds(source, 1), :]).astype(jnp.bfloat16)
        weight = query_ref[pl.ds(pl.multiple_of(source * wide, wide), wide), :]
        queries += jnp.dot(normed, weight, preferred_element_type=jnp.float32)
    queries = queries.astype(jnp.bfloat16)

    owned, visual, width = keys[0].shape
    columns = owned * visual
    factor = width ** (-0.5)
    wanted = wanted_ref[:, :1]
    scores, matches = [], []
    largest = jnp.full((rows, 1), -1e30, jnp.float32)
    for k in range(mp):
        first = jnp.bitwise_xor(place_ref[1], k) * owned
        slot = lax.broadcasted_iota(jnp.int32, (1, columns), 1) // visual + first
        match = wanted == slot
        score = lax.dot_general(
            queries,
            keys[k][...].reshape(columns, width),
            (((1,), (1,)), ((), ())),
            preferred_element_type=jnp.float32,
        )
        score = jnp.where(match, score * factor, -1e30)
        largest = jnp.maximum(largest, jnp.max(score, axis=1, keepdims=True))
        scores.append(score)
        matches.append(match)
    expo = [jnp.where(m, jnp.exp(s - largest), 0.0) for s, m in zip(scores, matches)]
    totals = sum(jnp.sum(e, axis=1, keepdims=True) for e in expo)
    result = jnp.zeros((rows, width), jnp.float32)
    for k in range(mp):
        rounded = (expo[k] / totals).astype(jnp.bfloat16)
        result += jnp.dot(
            rounded, values[k][...].reshape(columns, width), preferred_element_type=jnp.float32
        )
    out_ref[...] = result.astype(jnp.bfloat16)


def mix_kernel(dp, place_ref, gate_ref, *refs):
    groups, (weight_ref, token_ref, out_ref) = refs[:-3], refs[-3:]
    width = groups[0].shape[2]
    total = jnp.zeros(out_ref.shape, jnp.float32)
    for j, i, source in sources(place_ref[0], dp):
        weight = weight_ref[pl.ds(pl.multiple_of(source * width, width), width), :]
        total += jnp.dot(groups[j][i], weight, preferred_element_type=jnp.float32)
    gate = jnp.tanh(jnp.full((1, out_ref.shape[1]), gate_ref[0], jnp.float32))
    out_ref[...] = (token_ref[...].astype(jnp.float32) + gate * total).astype(jnp.bfloat16)


def body(
    dp,
    mp,
    tokens,
    norm_gain,
    query_weight,
    out_weight,
    gate_scalar,
    image_keys,
    image_values,
    active_image,
    image_slot,
):
    rows, wide = tokens.shape
    place = jnp.stack([lax.axis_index("dp"), lax.axis_index("mp")]).astype(jnp.int32)
    groups = gather(tokens, "dp", dp)
    keys = [image_keys] + [exchange(image_keys, "mp", mp, k) for k in range(1, mp)]
    values = [image_values] + [exchange(image_values, "mp", mp, k) for k in range(1, mp)]
    wanted = pl.pallas_call(
        slot_kernel,
        out_shape=jax.ShapeDtypeStruct((rows, 128), jnp.int32),
        in_specs=[SMEM, SMEM, SMEM],
        out_specs=VMEM,
        compiler_params=pltpu.CompilerParams(vmem_limit_bytes=1 << 20),
        name="slots",
    )(place, active_image, image_slot)
    attended = pl.pallas_call(
        functools.partial(attend_kernel, dp, mp),
        out_shape=jax.ShapeDtypeStruct((rows, query_weight.shape[1]), jnp.bfloat16),
        in_specs=[SMEM] + [VMEM] * (len(groups) + 3 + 2 * mp),
        out_specs=VMEM,
        compiler_params=pltpu.CompilerParams(vmem_limit_bytes=16 << 20),
        name="attend",
    )(place, *groups, norm_gain.reshape(dp, wide), query_weight, wanted, *keys, *values)
    heads = gather(attended, "dp", dp)
    return pl.pallas_call(
        functools.partial(mix_kernel, dp),
        out_shape=jax.ShapeDtypeStruct(tokens.shape, tokens.dtype),
        in_specs=[SMEM, SMEM] + [VMEM] * (len(heads) + 2),
        out_specs=VMEM,
        compiler_params=pltpu.CompilerParams(vmem_limit_bytes=8 << 20),
        name="mix",
    )(place, gate_scalar, *heads, out_weight, tokens)


def solution(mesh):
    in_specs = (
        P("mp", "dp"),
        P(),
        P(None, "dp"),
        P(None, "dp"),
        P(),
        P("mp", None, "dp"),
        P("mp", None, "dp"),
        P(),
        P(),
    )
    out_specs = P("mp", "dp")
    step = functools.partial(body, mesh.shape["dp"], mesh.shape["mp"])
    return jax.shard_map(step, mesh=mesh, in_specs=in_specs, out_specs=out_specs, check_vma=False)
```

```python
import functools

import jax
import jax.numpy as jnp
from jax import lax
from jax.experimental import pallas as pl
from jax.experimental.pallas import tpu as pltpu
from jax.sharding import PartitionSpec as P

epsilon = 1e-05


VMEM = pl.BlockSpec(memory_space=pltpu.VMEM)
SMEM = pl.BlockSpec(memory_space=pltpu.SMEM)
HBM = pl.BlockSpec(memory_space=pltpu.HBM)


def masks(size):
    low = 1 << ((size.bit_length() - 1) // 2)
    far = list(range(low, size, low))
    return far[0], far[1:], list(reversed(range(1, low)))


def exchange(x, axis, size, mask):
    return lax.ppermute(x, axis, [(i, i ^ mask) for i in range(size)])


def gather_wide(x, size):
    first, rest, near = masks(size)
    far = [exchange(x, "dp", size, m) for m in rest]
    head = exchange(x, "dp", size, first)
    side = jnp.stack([exchange(x, "dp", size, m) for m in near])
    far = jnp.stack(far)
    spread = [exchange(far, "dp", size, m) for m in near]
    last = exchange(side, "dp", size, first)
    arrays = [head[None], far, side, *spread, last]
    places = [[first], rest, near, *[[m ^ r for r in rest] for m in near], [first ^ m for m in near]]
    return arrays, places


def gather_small(x, size):
    first, rest, near = masks(size)
    far = [exchange(x, "dp", size, m) for m in rest + [first]]
    column = jnp.stack([x, *far])
    own = [0, *rest, first]
    spread = [exchange(column, "dp", size, m) for m in near]
    return [column, *spread], [own, *[[m ^ o for o in own] for m in near]]


def load_kernel(place_ref, active_ref, slot_ref, *refs):
    count = (len(refs) - 1) // 2
    out_ref, sem = refs[count], refs[-1]
    copies = [
        pltpu.make_async_copy(source, target, sem.at[i])
        for i, (source, target) in enumerate(zip(refs[:count], refs[count + 1 : -1]))
    ]
    for copy in copies:
        copy.start()
    steps = active_ref.shape[0]
    rows, lane = out_ref.shape
    base = place_ref[1] * (rows // steps)
    index = lax.broadcasted_iota(jnp.int32, (8, lane), 0)
    for tile in range(rows // 8):
        block = jnp.zeros((8, lane), jnp.int32)
        for r in range(8):
            row = tile * 8 + r
            block = jnp.where(index == r, slot_ref[active_ref[row % steps, base + row // steps]], block)
        out_ref[tile * 8 : tile * 8 + 8, :] = block
    for copy in copies:
        copy.wait()


def attend_kernel(places, mp, place_ref, *refs):
    tiles = len(places)
    groups, refs = refs[:tiles], refs[tiles:]
    gain_ref, query_ref, wanted_ref = refs[:3]
    keys, values = refs[3 : 3 + mp], refs[3 + mp : 3 + 2 * mp]
    out_ref = refs[-1]
    _, rows, wide = groups[0].shape
    chunks = wide // 128
    order = [(g, i, place) for g, at in zip(groups, places) for i, place in enumerate(at)]
    model = len(order) * wide

    def chunk(g, i, c):
        return g[i, :, c * 128 : c * 128 + 128].astype(jnp.float32)

    total = jnp.zeros((rows, 128), jnp.float32)
    for g, i, _ in order:
        for c in range(chunks):
            total += chunk(g, i, c)
    average = jnp.sum(total, axis=1, keepdims=True) * (1.0 / model)
    total = jnp.zeros((rows, 128), jnp.float32)
    for g, i, _ in order:
        for c in range(chunks):
            centred = chunk(g, i, c) - average
            total += centred * centred
    variance = jnp.sum(total, axis=1, keepdims=True) * (1.0 / model)
    scale = lax.rsqrt(variance + epsilon)

    queries = jnp.zeros((rows, out_ref.shape[1]), jnp.float32)
    for g, i, place in order:
        source = jnp.bitwise_xor(place_ref[0], place)
        normed = [
            ((chunk(g, i, c) - average) * scale * gain_ref[pl.ds(source * chunks + c, 1), :]).astype(jnp.bfloat16)
            for c in range(chunks)
        ]
        weight = query_ref[pl.ds(pl.multiple_of(source * wide, wide), wide), :]
        queries += jnp.dot(jnp.concatenate(normed, axis=1), weight, preferred_element_type=jnp.float32)
    queries = queries.astype(jnp.bfloat16)

    owned, visual, width = keys[0].shape
    columns = owned * visual
    factor = width ** (-0.5)
    wanted = wanted_ref[:, :1]
    scores, matches = [], []
    largest = jnp.full((rows, 1), -1e30, jnp.float32)
    for k in range(mp):
        begin = jnp.bitwise_xor(place_ref[1], k) * owned
        slot = lax.broadcasted_iota(jnp.int32, (1, columns), 1) // visual + begin
        match = wanted == slot
        score = lax.dot_general(
            queries,
            keys[k][...].reshape(columns, width),
            (((1,), (1,)), ((), ())),
            preferred_element_type=jnp.float32,
        )
        score = jnp.where(match, score * factor, -1e30)
        largest = jnp.maximum(largest, jnp.max(score, axis=1, keepdims=True))
        scores.append(score)
        matches.append(match)
    expo = [jnp.where(m, jnp.exp(s - largest), 0.0) for s, m in zip(scores, matches)]
    totals = sum(jnp.sum(e, axis=1, keepdims=True) for e in expo)
    result = jnp.zeros((rows, width), jnp.float32)
    for k in range(mp):
        rounded = (expo[k] / totals).astype(jnp.bfloat16)
        result += jnp.dot(
            rounded, values[k][...].reshape(columns, width), preferred_element_type=jnp.float32
        )
    out_ref[...] = result.astype(jnp.bfloat16)


def project(places, me, groups, weight_ref):
    width = groups[0].shape[2]
    total = None
    for g, at in zip(groups, places):
        for i, place in enumerate(at):
            source = jnp.bitwise_xor(me, place)
            weight = weight_ref[pl.ds(pl.multiple_of(source * width, width), width), :]
            part = jnp.dot(g[i], weight, preferred_element_type=jnp.float32)
            total = part if total is None else total + part
    return total


def own_kernel(places, place_ref, group_ref, weight_ref, out_ref):
    out_ref[...] = project(places, place_ref[0], [group_ref], weight_ref)


def mix_kernel(places, place_ref, gate_ref, *refs):
    groups, (partial_ref, weight_ref, token_ref, out_ref) = refs[:-4], refs[-4:]
    total = partial_ref[...] + project(places, place_ref[0], groups, weight_ref)
    gate = jnp.tanh(jnp.full((1, out_ref.shape[1]), gate_ref[0], jnp.float32))
    out_ref[...] = (token_ref[...].astype(jnp.float32) + gate * total).astype(jnp.bfloat16)


def kernel_call(kernel, limit, shape, in_specs, args, scratch=()):
    return pl.pallas_call(
        kernel,
        out_shape=shape,
        in_specs=in_specs,
        out_specs=jax.tree.map(lambda _: VMEM, shape),
        scratch_shapes=list(scratch),
        compiler_params=pltpu.CompilerParams(vmem_limit_bytes=limit << 20),
    )(*args)


def body(
    dp,
    mp,
    tokens,
    norm_gain,
    query_weight,
    out_weight,
    gate_scalar,
    image_keys,
    image_values,
    active_image,
    image_slot,
):
    rows, _ = tokens.shape
    place = jnp.stack([lax.axis_index("dp"), lax.axis_index("mp")]).astype(jnp.int32)
    arrays, places = gather_wide(tokens, dp)
    keys = [exchange(image_keys, "mp", mp, k) for k in range(1, mp)]
    values = [exchange(image_values, "mp", mp, k) for k in range(1, mp)]

    like = lambda x: jax.ShapeDtypeStruct(x.shape, x.dtype)
    loaded = (tokens, query_weight, image_keys, image_values)
    wanted, own, weight, own_keys, own_values = kernel_call(
        load_kernel,
        1,
        (jax.ShapeDtypeStruct((rows, 128), jnp.int32), *map(like, loaded)),
        [SMEM] * 3 + [HBM] * len(loaded),
        (place, active_image.T, image_slot, *[pltpu.with_memory_space_constraint(x, pltpu.HBM) for x in loaded]),
        [pltpu.SemaphoreType.DMA((len(loaded),))],
    )
    attended = kernel_call(
        functools.partial(attend_kernel, [[0], *places], mp),
        16,
        jax.ShapeDtypeStruct((rows, query_weight.shape[1]), jnp.bfloat16),
        [SMEM] + [VMEM] * (len(arrays) + 4 + 2 * mp),
        (place, own[None], *arrays, norm_gain.reshape(-1, 128), weight, wanted, own_keys, *keys, own_values, *values),
    )
    heads, places = gather_small(attended, dp)
    partial = kernel_call(
        functools.partial(own_kernel, places[:1]),
        4,
        jax.ShapeDtypeStruct(tokens.shape, jnp.float32),
        [SMEM] + [VMEM] * 2,
        (place, heads[0], out_weight),
    )
    return kernel_call(
        functools.partial(mix_kernel, places[1:]),
        4,
        like(tokens),
        [SMEM, SMEM] + [VMEM] * (len(heads) + 2),
        (place, gate_scalar, *heads[1:], partial, out_weight, tokens),
    )


def solution(mesh):
    dp, mp = mesh.shape["dp"], mesh.shape["mp"]
    in_specs = (
        P("mp", "dp"),
        P(),
        P(None, "dp"),
        P(None, "dp"),
        P(),
        P("mp", None, "dp"),
        P("mp", None, "dp"),
        P(),
        P(),
    )

    def step(*args):
        return body(dp, mp, *args)

    return jax.shard_map(step, mesh=mesh, in_specs=in_specs, out_specs=P("mp", "dp"), check_vma=False)
```

```python
import functools
import math

import jax
import jax.numpy as jnp
from jax import lax
from jax.experimental import pallas as pl
from jax.experimental.pallas import tpu as pltpu
from jax.sharding import PartitionSpec as P

epsilon = 1e-05
LOG2E = math.log2(math.e)
LOADED = 4
EARLY = 3


VMEM = pl.BlockSpec(memory_space=pltpu.VMEM)
SMEM = pl.BlockSpec(memory_space=pltpu.SMEM)
HBM = pl.BlockSpec(memory_space=pltpu.HBM)


def masks(size):
    low = 1 << ((size.bit_length() - 1) // 2)
    far = list(range(low, size, low))
    return far[0], far[1:], list(reversed(range(1, low)))


def exchange(x, axis, size, mask):
    return lax.ppermute(x, axis, [(i, i ^ mask) for i in range(size)])


def gather_wide(x, size):
    first, rest, near = masks(size)
    far = [exchange(x, "dp", size, m) for m in rest]
    head = exchange(x, "dp", size, first)
    side = jnp.stack([exchange(x, "dp", size, m) for m in near])
    far = jnp.stack(far)
    spread = [exchange(far, "dp", size, m) for m in near]
    last = exchange(side, "dp", size, first)
    arrays = [head[None], far, side, *spread, last]
    places = [[first], rest, near, *[[m ^ r for r in rest] for m in near], [first ^ m for m in near]]
    return arrays, places


def gather_small(x, size):
    first, rest, near = masks(size)
    far = {m: exchange(x, "dp", size, m) for m in [*reversed(rest), first]}
    column = jnp.stack([x, *[far[m] for m in [*rest, first]]])
    own = [0, *rest, first]
    spread = [exchange(column, "dp", size, m) for m in near]
    return [column, *spread], [own, *[[m ^ o for o in own] for m in near]]


def load_kernel(active_ref, slot_ref, *refs):
    count = LOADED
    sources, early = refs[:count], refs[count : -(count + 3)]
    wanted_ref, stats_ref, targets, sem = refs[-(count + 3)], refs[-(count + 2)], refs[-(count + 1) : -1], refs[-1]
    copies = [
        pltpu.make_async_copy(source, target, sem.at[i]) for i, (source, target) in enumerate(zip(sources, targets))
    ]
    for copy in copies:
        copy.start()
    steps = active_ref.shape[0]
    rows, lane = wanted_ref.shape
    base = lax.axis_index("mp") * (rows // steps)
    index = lax.broadcasted_iota(jnp.int32, (8, lane), 0)
    ahead = lax.broadcasted_iota(jnp.int32, (8, lane), 1) // targets[-1].shape[1]
    for tile in range(rows // 8):
        block = jnp.zeros((8, lane), jnp.int32)
        for r in range(8):
            row = tile * 8 + r
            block = jnp.where(index == r, slot_ref[active_ref[row % steps, base + row // steps]], block)
        wanted_ref[tile * 8 : tile * 8 + 8, :] = block - ahead
    copies[0].wait()
    tiles = [targets[0], *[g.at[i] for g in early for i in range(g.shape[0])]]
    wide = tiles[0].shape[1]
    zeros = jnp.zeros((rows, lane), jnp.float32)

    def add(c, total):
        for tile in tiles:
            total += tile[:, pl.ds(pl.multiple_of(c * lane, lane), lane)].astype(jnp.float32)
        return total

    average = jnp.sum(lax.fori_loop(0, wide // lane, add, zeros), axis=1, keepdims=True) * (1.0 / (len(tiles) * wide))

    def square(c, total):
        for tile in tiles:
            centred = tile[:, pl.ds(pl.multiple_of(c * lane, lane), lane)].astype(jnp.float32) - average
            total += centred * centred
        return total

    stats_ref[0] = jnp.broadcast_to(average, (rows, lane))
    stats_ref[1] = lax.fori_loop(0, wide // lane, square, zeros)
    for copy in copies[1:]:
        copy.wait()


def attend_kernel(places, early, mp, *refs):
    tiles = len(places)
    groups, refs = refs[:tiles], refs[tiles:]
    gain_ref, query_ref, wanted_ref, stats_ref = refs[:4]
    keys, values = refs[4 : 4 + mp], refs[4 + mp : 4 + 2 * mp]
    out_ref = refs[-1]
    _, rows, wide = groups[0].shape
    lane = 128
    chunks = wide // lane
    order = [(g, i, place) for g, at in zip(groups, places) for i, place in enumerate(at)]
    late = [(g, i) for g in groups[early:] for i in range(g.shape[0])]
    model = len(order) * wide
    me = lax.axis_index("dp")

    shift = stats_ref[0]
    zeros = jnp.zeros((rows, lane), jnp.float32)

    def gather_stats(c, carry):
        total, squares = carry
        for g, i in late:
            moved = g[i, :, pl.ds(pl.multiple_of(c * lane, lane), lane)].astype(jnp.float32) - shift
            total += moved
            squares += moved * moved
        return total, squares

    total, squares = lax.fori_loop(0, chunks, gather_stats, (zeros, stats_ref[1]))
    offset = jnp.sum(total, axis=1, keepdims=True) * (1.0 / model)
    variance = jnp.sum(squares, axis=1, keepdims=True) * (1.0 / model) - offset * offset
    average = shift + offset
    scale = jnp.broadcast_to(lax.rsqrt(variance + epsilon), (rows, lane))

    queries = jnp.zeros((rows, out_ref.shape[1]), jnp.float32)
    for g, i, place in order:
        source = jnp.bitwise_xor(me, place)
        normed = []
        for c in range(chunks):
            centred = g[i, :, c * lane : c * lane + lane].astype(jnp.float32) - average
            normed.append((centred * scale * gain_ref[pl.ds(source * chunks + c, 1), :]).astype(jnp.bfloat16))
        weight = query_ref[pl.ds(pl.multiple_of(source * wide, wide), wide), :]
        queries += jnp.dot(jnp.concatenate(normed, axis=1), weight, preferred_element_type=jnp.float32)
    queries = queries.astype(jnp.bfloat16)

    owned, visual, width = keys[0].shape
    columns = owned * visual
    factor = width ** (-0.5) * LOG2E
    wanted = wanted_ref[...]
    scores = []
    largest = jnp.full((rows, lane), -1e30, jnp.float32)
    for k in range(mp):
        begin = jnp.bitwise_xor(lax.axis_index("mp"), k) * owned
        score = lax.dot_general(
            queries,
            keys[k][...].reshape(columns, width),
            (((1,), (1,)), ((), ())),
            preferred_element_type=jnp.float32,
        )
        for j in range(columns // lane):
            match = wanted == begin + j * (lane // visual)
            part = jnp.where(match, score[:, j * lane : j * lane + lane], -1e30)
            largest = jnp.maximum(largest, part)
            scores.append(part)
    largest = jnp.broadcast_to(jnp.max(largest, axis=1, keepdims=True), (rows, lane))
    expo = [jnp.exp2((part - largest) * factor) for part in scores]
    share = 1.0 / jnp.sum(sum(expo), axis=1, keepdims=True)
    share = jnp.broadcast_to(share, (rows, lane))
    result = jnp.zeros((rows, width), jnp.float32)
    for k in range(mp):
        parts = expo[k * (columns // lane) : (k + 1) * (columns // lane)]
        rounded = jnp.concatenate([(part * share).astype(jnp.bfloat16) for part in parts], axis=1)
        result += jnp.dot(rounded, values[k][...].reshape(columns, width), preferred_element_type=jnp.float32)
    out_ref[...] = result.astype(jnp.bfloat16)


def project(places, groups, weight_ref):
    width = groups[0].shape[2]
    total = None
    for g, at in zip(groups, places):
        for i, place in enumerate(at):
            source = jnp.bitwise_xor(lax.axis_index("dp"), place)
            weight = weight_ref[pl.ds(pl.multiple_of(source * width, width), width), :]
            part = jnp.dot(g[i], weight, preferred_element_type=jnp.float32)
            total = part if total is None else total + part
    return total


def own_kernel(places, gate_ref, group_ref, weight_ref, token_ref, out_ref, tanh_ref):
    gate = jnp.tanh(jnp.full((1, out_ref.shape[1]), gate_ref[0], jnp.float32))
    out_ref[...] = token_ref[...].astype(jnp.float32) + gate * project(places, [group_ref], weight_ref)
    tanh_ref[...] = jnp.broadcast_to(gate, tanh_ref.shape)


def mix_kernel(places, *refs):
    groups, (partial_ref, tanh_ref, weight_ref, out_ref) = refs[:-4], refs[-4:]
    total = project(places, groups, weight_ref)
    out_ref[...] = (partial_ref[...] + tanh_ref[:1, :] * total).astype(jnp.bfloat16)


def kernel_call(kernel, limit, shape, in_specs, args, scratch=()):
    return pl.pallas_call(
        kernel,
        out_shape=shape,
        in_specs=in_specs,
        out_specs=jax.tree.map(lambda _: VMEM, shape),
        scratch_shapes=list(scratch),
        compiler_params=pltpu.CompilerParams(vmem_limit_bytes=limit << 20),
    )(*args)


def body(
    dp,
    mp,
    tokens,
    norm_gain,
    query_weight,
    out_weight,
    gate_scalar,
    image_keys,
    image_values,
    active_image,
    image_slot,
):
    rows = tokens.shape[0]
    arrays, places = gather_wide(tokens, dp)
    keys = [exchange(image_keys, "mp", mp, k) for k in range(1, mp)]
    values = [exchange(image_values, "mp", mp, k) for k in range(1, mp)]

    like = lambda x: jax.ShapeDtypeStruct(x.shape, x.dtype)
    floats = lambda *shape: jax.ShapeDtypeStruct(shape, jnp.float32)
    loaded = (tokens, query_weight, image_keys, image_values)
    wanted, stats, own, weight, own_keys, own_values = kernel_call(
        load_kernel,
        1,
        (jax.ShapeDtypeStruct((rows, 128), jnp.int32), floats(2, rows, 128), *map(like, loaded)),
        [SMEM] * 2 + [HBM] * LOADED + [VMEM] * EARLY,
        (active_image.T, image_slot, *[pltpu.with_memory_space_constraint(x, pltpu.HBM) for x in loaded], *arrays[:EARLY]),
        [pltpu.SemaphoreType.DMA((LOADED,))],
    )
    attended = kernel_call(
        functools.partial(attend_kernel, [[0], *places], EARLY + 1, mp),
        16,
        jax.ShapeDtypeStruct((rows, query_weight.shape[1]), jnp.bfloat16),
        [VMEM] * (len(arrays) + 5 + 2 * mp),
        (own[None], *arrays, norm_gain.reshape(-1, 128), weight, wanted, stats, own_keys, *keys, own_values, *values),
    )
    heads, places = gather_small(attended, dp)
    partial, gate = kernel_call(
        functools.partial(own_kernel, places[:1]),
        4,
        (floats(*tokens.shape), floats(8, tokens.shape[1])),
        [SMEM] + [VMEM] * 3,
        (gate_scalar, heads[0], out_weight, tokens),
    )
    return kernel_call(
        functools.partial(mix_kernel, places[1:]),
        4,
        like(tokens),
        [VMEM] * (len(heads) + 2),
        (*heads[1:], partial, gate, out_weight),
    )


def solution(mesh):
    dp, mp = mesh.shape["dp"], mesh.shape["mp"]
    in_specs = (
        P("mp", "dp"),
        P(),
        P(None, "dp"),
        P(None, "dp"),
        P(),
        P("mp", None, "dp"),
        P("mp", None, "dp"),
        P(),
        P(),
    )

    def step(*args):
        return body(dp, mp, *args)

    return jax.shard_map(step, mesh=mesh, in_specs=in_specs, out_specs=P("mp", "dp"), check_vma=False)
```

```python
import functools
import math

import jax
import jax.numpy as jnp
from jax import lax
from jax.experimental import pallas as pl
from jax.experimental.pallas import tpu as pltpu
from jax.sharding import PartitionSpec as P

epsilon = 1e-05
LOG2E = math.log2(math.e)
LOADED = 7
EARLY = 3


VMEM = pl.BlockSpec(memory_space=pltpu.VMEM)
SMEM = pl.BlockSpec(memory_space=pltpu.SMEM)
HBM = pl.BlockSpec(memory_space=pltpu.HBM)


def masks(size):
    low = 1 << ((size.bit_length() - 1) // 2)
    far = list(range(low, size, low))
    return far[0], far[1:], list(reversed(range(1, low)))


def exchange(x, axis, size, mask):
    return lax.ppermute(x, axis, [(i, i ^ mask) for i in range(size)])


def gather_wide(x, size):
    first, rest, near = masks(size)
    far = [exchange(x, "dp", size, m) for m in rest]
    head = exchange(x, "dp", size, first)
    side = jnp.stack([exchange(x, "dp", size, m) for m in near])
    far = jnp.stack(far)
    spread = [exchange(far, "dp", size, m) for m in near]
    last = exchange(side, "dp", size, first)
    arrays = [head[None], far, side, *spread, last]
    places = [[first], rest, near, *[[m ^ r for r in rest] for m in near], [first ^ m for m in near]]
    return arrays, places


def gather_small(x, size):
    first, rest, near = masks(size)
    far = {m: exchange(x, "dp", size, m) for m in [*reversed(rest), first]}
    column = jnp.stack([x, *[far[m] for m in [*rest, first]]])
    own = [0, *rest, first]
    spread = [exchange(column, "dp", size, m) for m in near]
    return [column, *spread], [own, *[[m ^ o for o in own] for m in near]]


def rows_of(weight_ref, source, count):
    return weight_ref[pl.ds(pl.multiple_of(source * count, count), count), :]


def load_kernel(*refs):
    early, sources = refs[:EARLY], refs[EARLY : EARLY + LOADED]
    wanted_ref, stats_ref, *targets = refs[EARLY + LOADED : EARLY + 2 * LOADED]
    active_ref, slot_ref, sem = refs[-3:]
    targets += [active_ref, slot_ref]
    copies = [
        pltpu.make_async_copy(source, target, sem.at[i]) for i, (source, target) in enumerate(zip(sources, targets))
    ]
    for copy in copies:
        copy.start()
    own_ref, visual = targets[0], targets[2].shape[1]
    rows, lane = wanted_ref.shape
    wide = own_ref.shape[1]

    copies[0].wait()
    tiles = [own_ref, *[g.at[i] for g in early for i in range(g.shape[0])]]
    zeros = jnp.zeros((rows, lane), jnp.float32)

    def add(c, total):
        for tile in tiles:
            total += tile[:, pl.ds(pl.multiple_of(c * lane, lane), lane)].astype(jnp.float32)
        return total

    average = jnp.sum(lax.fori_loop(0, wide // lane, add, zeros), axis=1, keepdims=True) * (1.0 / (len(tiles) * wide))
    shift = jnp.broadcast_to(average, (rows, lane))
    stats_ref[0] = shift

    for copy in copies[-2:]:
        copy.wait()
    steps = active_ref.shape[0]
    base = lax.axis_index("mp") * (rows // steps)
    index = lax.broadcasted_iota(jnp.int32, (8, lane), 0)
    ahead = lax.broadcasted_iota(jnp.int32, (8, lane), 1) // visual
    for group in range(rows // 8):
        block = jnp.zeros((8, lane), jnp.int32)
        for r in range(8):
            row = group * 8 + r
            block = jnp.where(index == r, slot_ref[active_ref[row % steps, base + row // steps]], block)
        wanted_ref[group * 8 : group * 8 + 8, :] = block - ahead

    squares = zeros
    for tile in tiles:
        for c in range(wide // lane):
            moved = tile[:, c * lane : c * lane + lane].astype(jnp.float32) - shift
            squares += moved * moved
    stats_ref[1] = squares
    for copy in copies[1:-2]:
        copy.wait()


def attend_kernel(places, early, mp, *refs):
    tiles = len(places)
    groups, refs = refs[:tiles], refs[tiles:]
    gain_ref, weight_ref, wanted_ref, stats_ref = refs[:4]
    keys, values = refs[4 : 4 + mp], refs[4 + mp : 4 + 2 * mp]
    out_ref = refs[-1]
    _, rows, wide = groups[0].shape
    lane = wanted_ref.shape[1]
    chunks = wide // lane
    model = weight_ref.shape[0]
    late = [g.at[i] for g in groups[early:] for i in range(g.shape[0])]

    shift = stats_ref[0]

    def add(c, carry):
        total, squares = carry
        for tile in late:
            moved = tile[:, pl.ds(pl.multiple_of(c * lane, lane), lane)].astype(jnp.float32) - shift
            total += moved
            squares += moved * moved
        return total, squares

    total, squares = lax.fori_loop(0, chunks, add, (jnp.zeros((rows, lane), jnp.float32), stats_ref[1]))
    offset = jnp.sum(total, axis=1, keepdims=True) * (1.0 / model)
    variance = jnp.sum(squares, axis=1, keepdims=True) * (1.0 / model) - offset * offset
    average = shift + offset
    scale = jnp.broadcast_to(lax.rsqrt(variance + epsilon), (rows, lane))

    queries = jnp.zeros((rows, out_ref.shape[1]), jnp.float32)
    for g, at in zip(groups, places):
        for i, place in enumerate(at):
            source = jnp.bitwise_xor(lax.axis_index("dp"), place)
            normed = []
            for c in range(chunks):
                centred = g[i, :, c * lane : c * lane + lane].astype(jnp.float32) - average
                normed.append((centred * scale * gain_ref[pl.ds(source * chunks + c, 1), :]).astype(jnp.bfloat16))
            weight = rows_of(weight_ref, source, wide)
            queries += jnp.dot(jnp.concatenate(normed, axis=1), weight, preferred_element_type=jnp.float32)
    queries = queries.astype(jnp.bfloat16)

    owned, visual, width = keys[0].shape
    columns = owned * visual
    factor = width ** (-0.5) * LOG2E
    wanted = wanted_ref[...]
    peaks, sums, expos = [], [], []
    for k in range(mp):
        begin = jnp.bitwise_xor(lax.axis_index("mp"), k) * owned
        score = lax.dot_general(
            queries,
            keys[k][...].reshape(columns, width),
            (((1,), (1,)), ((), ())),
            preferred_element_type=jnp.float32,
        )
        parts = []
        for j in range(columns // lane):
            match = wanted == begin + j * (lane // visual)
            parts.append(jnp.where(match, score[:, j * lane : j * lane + lane], -1e30))
        peak = jnp.max(functools.reduce(jnp.maximum, parts), axis=1, keepdims=True)
        spread = jnp.broadcast_to(peak, (rows, lane))
        expo = [jnp.exp2((part - spread) * factor) for part in parts]
        peaks.append(peak)
        sums.append(jnp.sum(functools.reduce(jnp.add, expo), axis=1, keepdims=True))
        expos.append(expo)
    peak = functools.reduce(jnp.maximum, peaks)
    weights = [jnp.exp2((p - peak) * factor) for p in peaks]
    share = 1.0 / functools.reduce(jnp.add, [w * t for w, t in zip(weights, sums)])
    result = jnp.zeros((rows, width), jnp.float32)
    for k in range(mp):
        times = jnp.broadcast_to(weights[k] * share, (rows, lane))
        rounded = jnp.concatenate([(part * times).astype(jnp.bfloat16) for part in expos[k]], axis=1)
        result += jnp.dot(rounded, values[k][...].reshape(columns, width), preferred_element_type=jnp.float32)
    out_ref[...] = result.astype(jnp.bfloat16)


def project(places, one, two, weight_ref):
    width = one.shape[2]
    me = lax.axis_index("dp")
    total = None
    for i, place in enumerate(places):
        even = jnp.bitwise_and(jnp.bitwise_xor(me, place), 1) == 0
        pair = jnp.concatenate([jnp.where(even, one[i], two[i]), jnp.where(even, two[i], one[i])], axis=1)
        weight = rows_of(weight_ref, jnp.right_shift(jnp.bitwise_xor(me, place), 1), 2 * width)
        part = jnp.dot(pair, weight, preferred_element_type=jnp.float32)
        total = part if total is None else total + part
    return total


def middle_kernel(places, gate_ref, *refs):
    groups, (weight_ref, token_ref, out_ref, tanh_ref) = refs[:-4], refs[-4:]
    gate = jnp.tanh(jnp.full((1, out_ref.shape[1]), gate_ref[0], jnp.float32))
    total = functools.reduce(
        jnp.add, [project(at, groups[2 * i], groups[2 * i + 1], weight_ref) for i, at in enumerate(places)]
    )
    out_ref[...] = token_ref[...].astype(jnp.float32) + gate * total
    tanh_ref[...] = jnp.broadcast_to(gate, tanh_ref.shape)


def mix_kernel(places, own_ref, last_ref, partial_ref, tanh_ref, weight_ref, out_ref):
    total = project(places, own_ref, last_ref, weight_ref)
    out_ref[...] = (partial_ref[...] + tanh_ref[:1, :] * total).astype(jnp.bfloat16)


def kernel_call(kernel, limit, shape, in_specs, args, scratch=()):
    return pl.pallas_call(
        kernel,
        out_shape=shape,
        in_specs=in_specs,
        out_specs=jax.tree.map(lambda _: VMEM, shape),
        scratch_shapes=list(scratch),
        compiler_params=pltpu.CompilerParams(vmem_limit_bytes=limit << 20),
    )(*args)


def body(
    dp,
    mp,
    tokens,
    norm_gain,
    query_weight,
    out_weight,
    gate_scalar,
    image_keys,
    image_values,
    active_image,
    image_slot,
):
    rows = tokens.shape[0]
    arrays, places = gather_wide(tokens, dp)
    keys = [exchange(image_keys, "mp", mp, k) for k in range(1, mp)]
    values = [exchange(image_values, "mp", mp, k) for k in range(1, mp)]

    like = lambda x: jax.ShapeDtypeStruct(x.shape, x.dtype)
    floats = lambda *shape: jax.ShapeDtypeStruct(shape, jnp.float32)
    width = query_weight.shape[1]
    loaded = (tokens, query_weight, image_keys, image_values, norm_gain.reshape(-1, 128), active_image.T, image_slot)
    wanted, stats, own, weight, own_keys, own_values, gain = kernel_call(
        load_kernel,
        2,
        (jax.ShapeDtypeStruct((rows, 128), jnp.int32), floats(2, rows, 128), *map(like, loaded[:5])),
        [VMEM] * EARLY + [HBM] * LOADED,
        (*arrays[:EARLY], *[pltpu.with_memory_space_constraint(x, pltpu.HBM) for x in loaded]),
        [*[pltpu.SMEM(x.shape, x.dtype) for x in loaded[5:]], pltpu.SemaphoreType.DMA((LOADED,))],
    )
    attended = kernel_call(
        functools.partial(attend_kernel, [[0], *places], EARLY + 1, mp),
        16,
        jax.ShapeDtypeStruct((rows, width), jnp.bfloat16),
        [VMEM] * (len(arrays) + 5 + 2 * mp),
        (own[None], *arrays, gain, weight, wanted, stats, own_keys, *keys, own_values, *values),
    )
    heads, places = gather_small(attended, dp)
    pairs = [heads[i] for i in range(1, len(heads) - 1)]
    partial, gate = kernel_call(
        functools.partial(middle_kernel, places[1:-1:2]),
        4,
        (floats(*tokens.shape), floats(8, tokens.shape[1])),
        [SMEM] + [VMEM] * (len(pairs) + 2),
        (gate_scalar, *pairs, out_weight, tokens),
    )
    return kernel_call(
        functools.partial(mix_kernel, places[0]),
        4,
        like(tokens),
        [VMEM] * 5,
        (heads[0], heads[-1], partial, gate, out_weight),
    )


def solution(mesh):
    dp, mp = mesh.shape["dp"], mesh.shape["mp"]
    in_specs = (
        P("mp", "dp"),
        P(),
        P(None, "dp"),
        P(None, "dp"),
        P(),
        P("mp", None, "dp"),
        P("mp", None, "dp"),
        P(),
        P(),
    )

    def step(*args):
        return body(dp, mp, *args)

    return jax.shard_map(step, mesh=mesh, in_specs=in_specs, out_specs=P("mp", "dp"), check_vma=False)
```

```python
import functools
import math

import jax
import jax.numpy as jnp
from jax import lax
from jax.experimental import pallas as pl
from jax.experimental.pallas import tpu as pltpu
from jax.sharding import PartitionSpec as P

epsilon = 1e-05
LOG2E = math.log2(math.e)
LOADED = 7
EARLY = 3


VMEM = pl.BlockSpec(memory_space=pltpu.VMEM)
SMEM = pl.BlockSpec(memory_space=pltpu.SMEM)
HBM = pl.BlockSpec(memory_space=pltpu.HBM)


def masks(size):
    low = 1 << ((size.bit_length() - 1) // 2)
    far = list(range(low, size, low))
    return far[0], far[1:], list(reversed(range(1, low)))


def exchange(x, axis, size, mask):
    return lax.ppermute(x, axis, [(i, i ^ mask) for i in range(size)])


def gather_wide(x, size):
    first, rest, near = masks(size)
    far = [exchange(x, "dp", size, m) for m in rest]
    head = exchange(x, "dp", size, first)
    side = jnp.stack([exchange(x, "dp", size, m) for m in near])
    far = jnp.stack(far)
    spread = [exchange(far, "dp", size, m) for m in near]
    last = exchange(side, "dp", size, first)
    arrays = [head[None], far, side, *spread, last]
    places = [[first], rest, near, *[[m ^ r for r in rest] for m in near], [first ^ m for m in near]]
    return arrays, places


def gather_small(x, size):
    first, rest, near = masks(size)
    far = {m: exchange(x, "dp", size, m) for m in [*reversed(rest), first]}
    column = jnp.stack([x, *[far[m] for m in [*rest, first]]])
    own = [0, *rest, first]
    spread = [exchange(column, "dp", size, m) for m in near]
    return [column, *spread], [own, *[[m ^ o for o in own] for m in near]]


def rows_of(weight_ref, source, count):
    return weight_ref[pl.ds(pl.multiple_of(source * count, count), count), :]


def load_kernel(*refs):
    early, sources = refs[:EARLY], refs[EARLY : EARLY + LOADED]
    wanted_ref, stats_ref, *targets = refs[EARLY + LOADED : EARLY + 2 * LOADED]
    active_ref, slot_ref, sem = refs[-3:]
    targets += [active_ref, slot_ref]
    copies = [
        pltpu.make_async_copy(source, target, sem.at[i]) for i, (source, target) in enumerate(zip(sources, targets))
    ]
    for copy in copies:
        copy.start()
    own_ref, visual = targets[0], targets[2].shape[1]
    rows, lane = wanted_ref.shape
    wide = own_ref.shape[1]

    copies[0].wait()
    tiles = [own_ref, *[g.at[i] for g in early for i in range(g.shape[0])]]
    zeros = jnp.zeros((rows, lane), jnp.float32)

    def add(c, total):
        for tile in tiles:
            total += tile[:, pl.ds(pl.multiple_of(c * lane, lane), lane)].astype(jnp.float32)
        return total

    average = jnp.sum(lax.fori_loop(0, wide // lane, add, zeros), axis=1, keepdims=True) * (1.0 / (len(tiles) * wide))
    shift = jnp.broadcast_to(average, (rows, lane))
    stats_ref[0] = shift

    for copy in copies[-2:]:
        copy.wait()
    steps = active_ref.shape[0]
    base = lax.axis_index("mp") * (rows // steps)
    index = lax.broadcasted_iota(jnp.int32, (8, lane), 0)
    ahead = lax.broadcasted_iota(jnp.int32, (8, lane), 1) // visual
    for group in range(rows // 8):
        block = jnp.zeros((8, lane), jnp.int32)
        for r in range(8):
            row = group * 8 + r
            block = jnp.where(index == r, slot_ref[active_ref[row % steps, base + row // steps]], block)
        wanted_ref[group * 8 : group * 8 + 8, :] = block - ahead

    squares = zeros
    for tile in tiles:
        for c in range(wide // lane):
            moved = tile[:, c * lane : c * lane + lane].astype(jnp.float32) - shift
            squares += moved * moved
    stats_ref[1] = squares
    for copy in copies[1:-2]:
        copy.wait()


def deviations(tiles, shift, total, squares):
    lane = shift.shape[1]

    def add(c, carry):
        total, squares = carry
        for tile in tiles:
            moved = tile[:, pl.ds(pl.multiple_of(c * lane, lane), lane)].astype(jnp.float32) - shift
            total += moved
            squares += moved * moved
        return total, squares

    return lax.fori_loop(0, tiles[0].shape[1] // lane, add, (total, squares))


def lead_kernel(*refs):
    groups, (stats_ref, sums_ref) = refs[:-2], refs[-2:]
    tiles = [g.at[i] for g in groups for i in range(g.shape[0])]
    shift = stats_ref[0]
    total, squares = deviations(tiles, shift, jnp.zeros_like(shift), stats_ref[1])
    sums_ref[0] = shift
    sums_ref[1] = squares
    sums_ref[2] = total


def attend_kernel(places, early, mp, *refs):
    tiles = len(places)
    groups, refs = refs[:tiles], refs[tiles:]
    gain_ref, weight_ref, wanted_ref, stats_ref = refs[:4]
    keys, values = refs[4 : 4 + mp], refs[4 + mp : 4 + 2 * mp]
    out_ref = refs[-1]
    _, rows, wide = groups[0].shape
    lane = wanted_ref.shape[1]
    chunks = wide // lane
    model = weight_ref.shape[0]
    late = [g.at[i] for g in groups[early:-1] for i in range(g.shape[0])]

    shift = stats_ref[0]

    total, squares = deviations(late, shift, stats_ref[2], stats_ref[1])
    offset = jnp.sum(total, axis=1, keepdims=True) * (1.0 / model)
    variance = jnp.sum(squares, axis=1, keepdims=True) * (1.0 / model) - offset * offset
    average = shift + offset
    scale = jnp.broadcast_to(lax.rsqrt(variance + epsilon), (rows, lane))

    queries = jnp.zeros((rows, out_ref.shape[1]), jnp.float32)
    for g, at in zip(groups, places):
        for i, place in enumerate(at):
            source = jnp.bitwise_xor(lax.axis_index("dp"), place)
            normed = []
            for c in range(chunks):
                centred = g[i, :, c * lane : c * lane + lane].astype(jnp.float32) - average
                normed.append((centred * scale * gain_ref[pl.ds(source * chunks + c, 1), :]).astype(jnp.bfloat16))
            weight = rows_of(weight_ref, source, wide)
            queries += jnp.dot(jnp.concatenate(normed, axis=1), weight, preferred_element_type=jnp.float32)
    queries = queries.astype(jnp.bfloat16)

    owned, visual, width = keys[0].shape
    columns = owned * visual
    factor = width ** (-0.5) * LOG2E
    wanted = wanted_ref[...]
    peaks, sums, expos = [], [], []
    for k in range(mp):
        begin = jnp.bitwise_xor(lax.axis_index("mp"), k) * owned
        score = lax.dot_general(
            queries,
            keys[k][...].reshape(columns, width),
            (((1,), (1,)), ((), ())),
            preferred_element_type=jnp.float32,
        )
        parts = []
        for j in range(columns // lane):
            match = wanted == begin + j * (lane // visual)
            parts.append(jnp.where(match, score[:, j * lane : j * lane + lane], -1e30))
        peak = jnp.max(functools.reduce(jnp.maximum, parts), axis=1, keepdims=True)
        spread = jnp.broadcast_to(peak, (rows, lane))
        expo = [jnp.exp2((part - spread) * factor) for part in parts]
        peaks.append(peak)
        sums.append(jnp.sum(functools.reduce(jnp.add, expo), axis=1, keepdims=True))
        expos.append(expo)
    peak = functools.reduce(jnp.maximum, peaks)
    weights = [jnp.exp2((p - peak) * factor) for p in peaks]
    share = 1.0 / functools.reduce(jnp.add, [w * t for w, t in zip(weights, sums)])
    result = jnp.zeros((rows, width), jnp.float32)
    for k in range(mp):
        times = jnp.broadcast_to(weights[k] * share, (rows, lane))
        rounded = jnp.concatenate([(part * times).astype(jnp.bfloat16) for part in expos[k]], axis=1)
        result += jnp.dot(rounded, values[k][...].reshape(columns, width), preferred_element_type=jnp.float32)
    out_ref[...] = result.astype(jnp.bfloat16)


def project(places, one, two, weight_ref):
    width = one.shape[2]
    me = lax.axis_index("dp")
    total = None
    for i, place in enumerate(places):
        even = jnp.bitwise_and(jnp.bitwise_xor(me, place), 1) == 0
        pair = jnp.concatenate([jnp.where(even, one[i], two[i]), jnp.where(even, two[i], one[i])], axis=1)
        weight = rows_of(weight_ref, jnp.right_shift(jnp.bitwise_xor(me, place), 1), 2 * width)
        part = jnp.dot(pair, weight, preferred_element_type=jnp.float32)
        total = part if total is None else total + part
    return total


def middle_kernel(places, gate_ref, *refs):
    groups, (weight_ref, token_ref, out_ref, tanh_ref) = refs[:-4], refs[-4:]
    gate = jnp.tanh(jnp.full((1, out_ref.shape[1]), gate_ref[0], jnp.float32))
    total = functools.reduce(
        jnp.add, [project(at, groups[2 * i], groups[2 * i + 1], weight_ref) for i, at in enumerate(places)]
    )
    out_ref[...] = token_ref[...].astype(jnp.float32) + gate * total
    tanh_ref[...] = jnp.broadcast_to(gate, tanh_ref.shape)


def mix_kernel(places, own_ref, last_ref, partial_ref, tanh_ref, weight_ref, out_ref):
    total = project(places, own_ref, last_ref, weight_ref)
    out_ref[...] = (partial_ref[...] + tanh_ref[:1, :] * total).astype(jnp.bfloat16)


def kernel_call(kernel, limit, shape, in_specs, args, scratch=()):
    return pl.pallas_call(
        kernel,
        out_shape=shape,
        in_specs=in_specs,
        out_specs=jax.tree.map(lambda _: VMEM, shape),
        scratch_shapes=list(scratch),
        compiler_params=pltpu.CompilerParams(vmem_limit_bytes=limit << 20),
    )(*args)


def body(
    dp,
    mp,
    tokens,
    norm_gain,
    query_weight,
    out_weight,
    gate_scalar,
    image_keys,
    image_values,
    active_image,
    image_slot,
):
    rows = tokens.shape[0]
    arrays, places = gather_wide(tokens, dp)
    keys = [exchange(image_keys, "mp", mp, k) for k in range(1, mp)]
    values = [exchange(image_values, "mp", mp, k) for k in range(1, mp)]

    like = lambda x: jax.ShapeDtypeStruct(x.shape, x.dtype)
    floats = lambda *shape: jax.ShapeDtypeStruct(shape, jnp.float32)
    width = query_weight.shape[1]
    loaded = (tokens, query_weight, image_keys, image_values, norm_gain.reshape(-1, 128), active_image.T, image_slot)
    wanted, stats, own, weight, own_keys, own_values, gain = kernel_call(
        load_kernel,
        2,
        (jax.ShapeDtypeStruct((rows, 128), jnp.int32), floats(2, rows, 128), *map(like, loaded[:5])),
        [VMEM] * EARLY + [HBM] * LOADED,
        (*arrays[:EARLY], *[pltpu.with_memory_space_constraint(x, pltpu.HBM) for x in loaded]),
        [*[pltpu.SMEM(x.shape, x.dtype) for x in loaded[5:]], pltpu.SemaphoreType.DMA((LOADED,))],
    )
    ahead = [*range(EARLY, len(arrays) - 3), len(arrays) - 1]
    stats = kernel_call(
        lead_kernel, 2, floats(3, rows, 128), [VMEM] * (len(ahead) + 1), (*[arrays[i] for i in ahead], stats)
    )
    attended = kernel_call(
        functools.partial(attend_kernel, [[0], *places], len(arrays) - 2, mp),
        16,
        jax.ShapeDtypeStruct((rows, width), jnp.bfloat16),
        [VMEM] * (len(arrays) + 5 + 2 * mp),
        (own[None], *arrays, gain, weight, wanted, stats, own_keys, *keys, own_values, *values),
    )
    heads, places = gather_small(attended, dp)
    pairs = [heads[i] for i in range(1, len(heads) - 1)]
    partial, gate = kernel_call(
        functools.partial(middle_kernel, places[1:-1:2]),
        4,
        (floats(*tokens.shape), floats(8, tokens.shape[1])),
        [SMEM] + [VMEM] * (len(pairs) + 2),
        (gate_scalar, *pairs, out_weight, tokens),
    )
    return kernel_call(
        functools.partial(mix_kernel, places[0]),
        4,
        like(tokens),
        [VMEM] * 5,
        (heads[0], heads[-1], partial, gate, out_weight),
    )


def solution(mesh):
    dp, mp = mesh.shape["dp"], mesh.shape["mp"]
    in_specs = (
        P("mp", "dp"),
        P(),
        P(None, "dp"),
        P(None, "dp"),
        P(),
        P("mp", None, "dp"),
        P("mp", None, "dp"),
        P(),
        P(),
    )

    def step(*args):
        return body(dp, mp, *args)

    return jax.shard_map(step, mesh=mesh, in_specs=in_specs, out_specs=P("mp", "dp"), check_vma=False)
```
